128 devices in a mesh: row: 16 (over z, y), col: 8 (over x, core).
Axes of the slice: x: 4, y: 4, z: 4, core: 2. Of those that a mesh axis runs over, the one named last changes fastest.
Arguments:
- counts: int32 [2048, 262144], P('row', 'col'), may hold values from 0 to 7, as said below
- row_total: float32 [2048], P('row'), may hold values from 1 to 3670016, as said below
- col_total: float32 [262144], P('col'), may hold values from 1 to 3670272, as said below
- grand_total: float32 [1], replicated, as said below
- sketch: float32 [262144, 96], P(('col', 'row')), may hold values from -0.00024414062 to 0.00024414062
Outputs:
- column_factors: float32 [262144, 96], P(('col', 'row'))
- gram_factor: float32 [96, 96], replicated
The draws below stay inside these ranges and needn't reach their ends.
Inputs may be any that keep to these rules, and one draw needn't show every extreme that they name: About half of the counts are zero. `row_total`: each row's total is its counts' sum times a factor between 1 and 2. `col_total`: each item's total is its counts' sum over the slab plus one, times 262144 / 2048, times a factor between 1 and 2. `grand_total`: the grand total is the sum of col_total times a factor between 1 and 1.25.
All inputs are finite; a program needn't handle non-finite values.
Results may differ from the reference program's by a relative error of at most 0.0003.
Values sent between devices are 32-bit elements; how exact they have to be, the bound alone decides.
No kernel may reach another device: no remote copies, remote signals or barrier semaphores. Data moves between devices by JAX's collectives and lax.ppermute only.
A program may use at most 128 MiB of HBM per device.

```python
import math
import jax
import jax.numpy as jnp
from jax import lax

C = 262144
K = 96
ROWS = 2048


def shared_counts(key):
    drawn = jax.random.randint(jax.random.fold_in(key, 101), (ROWS, C), -6, 8)
    return jnp.maximum(drawn, 0).astype(jnp.int32)


def column_marginal(key):
    slab_sums = jnp.sum(shared_counts(key), axis=0).astype(jnp.float32) + 1.0
    factor = jax.random.uniform(jax.random.fold_in(key, 202), (C,), jnp.float32, 1.0, 2.0)
    return slab_sums * float(C // ROWS) * factor


def draw_counts(key, part):
    return shared_counts(key)


def draw_row_total(key, part):
    row_sums = jnp.sum(shared_counts(key), axis=1).astype(jnp.float32)
    factor = jax.random.uniform(jax.random.fold_in(key, 303), (ROWS,), jnp.float32, 1.0, 2.0)
    return jnp.maximum(row_sums, 1.0) * factor


def draw_col_total(key, part):
    return column_marginal(key)


def draw_grand_total(key, part):
    whole = jnp.sum(column_marginal(key))
    factor = jax.random.uniform(jax.random.fold_in(key, 404), (1,), jnp.float32, 1.0, 1.25)
    return whole * factor


def block_scale(rng, shape, split, low, largest):
    loudness = 1.0
    for axis_at, blocks in split:
        heights = jax.random.uniform(jax.random.fold_in(jax.random.fold_in(rng, 6), axis_at), (blocks,), jnp.float32, low / len(split), largest / len(split))
        loudness = loudness * jnp.repeat(jnp.exp(heights), shape[axis_at] // blocks).reshape((-1,) + (1,) * (len(shape) - 1 - axis_at))
    return loudness


def normal_values(rng, dims, deviation, limit, pieces=(), kind=jnp.bfloat16):
    values = jax.random.normal(rng, dims, jnp.float32) * deviation
    if len(pieces) > 0:
        values = block_scale(rng, dims, pieces, -0.22, 0.18) * values
    return jnp.clip(values, min=-limit, max=limit).astype(kind)


def setup_inputs(seed: int = 0) -> dict:
    seeds = jax.random.split(jax.random.key(seed), 6)
    return {
        "counts": draw_counts(jax.random.fold_in(seeds[5], 71), 0),
        "row_total": draw_row_total(jax.random.fold_in(seeds[5], 71), 0),
        "col_total": draw_col_total(jax.random.fold_in(seeds[5], 71), 0),
        "grand_total": draw_grand_total(jax.random.fold_in(seeds[5], 71), 0),
        "sketch": normal_values(seeds[4], (C, K), (C * ROWS) ** -0.5, 0.00024414062, ((0, 128),), jnp.float32),
    }


def ppmi_block(counts_block, row_log, col_block):
    counts_float = counts_block.astype(jnp.float32)
    pmi = jnp.log(jnp.maximum(counts_float, 1.0)) + row_log[:, None] - jnp.log(col_block)[None, :]
    return jnp.where(counts_block > 0, jnp.maximum(pmi, 0.0), 0.0)

def reference(counts, row_total, col_total, grand_total, sketch):
    block_width = math.gcd(C, 8192)
    block_count = C // block_width
    row_log = jnp.log(grand_total[0]) - jnp.log(row_total)
    blocks = jnp.arange(block_count, dtype=jnp.int32)

    def tile_of(block):
        offset = (block * block_width).astype(jnp.int32)
        counts_block = lax.dynamic_slice_in_dim(counts, offset, block_width, 1)
        col_block = lax.dynamic_slice_in_dim(col_total, offset, block_width, 0)
        return ppmi_block(counts_block, row_log, col_block)

    def add_block(running, block):
        offset = (block * block_width).astype(jnp.int32)
        sketch_block = lax.dynamic_slice_in_dim(sketch, offset, block_width, 0)
        return (running + jnp.dot(tile_of(block).astype(jnp.float32), sketch_block.astype(jnp.float32), precision=lax.Precision.HIGHEST, preferred_element_type=jnp.float32), None)
    image, _ = lax.scan(add_block, jnp.zeros((ROWS, K), jnp.float32), blocks)
    gram_matrix = jnp.dot(image.T.astype(jnp.float32), image.astype(jnp.float32), precision=lax.Precision.HIGHEST, preferred_element_type=jnp.float32)
    factor = jnp.linalg.cholesky(gram_matrix)
    basis = jax.scipy.linalg.solve_triangular(factor, image.T, lower=True).T

    def column_block(block):
        return jnp.dot(tile_of(block).T.astype(jnp.float32), basis.astype(jnp.float32), precision=lax.Precision.HIGHEST, preferred_element_type=jnp.float32)
    column_factors = lax.map(column_block, blocks).reshape(C, K)
    return (column_factors, factor)
```

```python
import functools

import jax
import jax.numpy as jnp
from jax import lax
from jax.experimental import pallas as pl
from jax.experimental.pallas import tpu as pltpu
from jax.sharding import Mesh
from jax.sharding import PartitionSpec as P


ROW = ("row_0", "row_1")
COL_ROW = ("col", "row_0", "row_1")
Z, Y = ROW
STEP = 512


def shift(array, axis, by):
    size = lax.axis_size(axis)
    return lax.ppermute(array, axis, [(i, (i + by) % size) for i in range(size)])


def add_partner(array, axis, bit):
    size = lax.axis_size(axis)
    return array + lax.ppermute(array, axis, [(i, i ^ bit) for i in range(size)])


def two_parts(x):
    high = x.astype(jnp.bfloat16)
    low = (x - high.astype(jnp.float32)).astype(jnp.bfloat16)
    return high, low


def ppmi_parts(counts_ref, col_ref, row_log):
    logs = jnp.log(counts_ref[...].astype(jnp.float32))
    ppmi = jnp.maximum(logs + row_log - jnp.log(col_ref[...]), 0.0)
    return jnp.concatenate(two_parts(ppmi), axis=0)


def image_kernel(buffers, index_ref, row_ref, start_ref, *refs):
    counts, cols, slabs = refs[:buffers], refs[buffers : 2 * buffers], refs[2 * buffers : 3 * buffers]
    out_ref, total = refs[3 * buffers :]
    step = pl.program_id(0)
    width, rows = start_ref.shape

    @pl.when(step == 0)
    def _():
        total[...] = jnp.zeros_like(total)

    row_log = row_ref[...]
    for counts_ref, col_ref, slab_ref in zip(counts, cols, slabs):
        ppmi = ppmi_parts(counts_ref, col_ref, row_log)
        slab = jnp.concatenate(two_parts(slab_ref[...]), axis=0)
        total[...] += lax.dot_general(
            slab, ppmi, (((1,), (1,)), ((), ())), preferred_element_type=jnp.float32
        )

    @pl.when(step == pl.num_programs(0) - 1)
    def _():
        cross = total[:width, rows:] + total[width:, :rows]
        out_ref[...] = start_ref[...] + (total[:width, :rows] + cross)


def columns_kernel(buffers, added, index_ref, row_ref, image_ref, *refs):
    counts, cols = refs[:buffers], refs[buffers : 2 * buffers]
    addends, outs = refs[2 * buffers : len(refs) - buffers], refs[len(refs) - buffers :]
    row_log = row_ref[...]
    high, low = two_parts(image_ref[...])
    image = jnp.concatenate(
        [
            jnp.concatenate([high, high], axis=1),
            jnp.concatenate([low, jnp.zeros_like(low)], axis=1),
        ],
        axis=0,
    )
    width = image_ref.shape[0]
    for at in range(buffers):
        ppmi = ppmi_parts(counts[at], cols[at], row_log)
        product = jnp.dot(image, ppmi, preferred_element_type=jnp.float32)
        value = product[:width] + product[width:]
        if added:
            value = value + addends[at][...]
        outs[at][...] = value


def counts_specs(buffers, blocks, per_block, rows):
    def at(buffer, height):
        def index_map(i, index):
            return (0, index[buffer * blocks + i // per_block] * per_block + i % per_block)

        return pl.BlockSpec((height, STEP), index_map)

    return [at(b, rows) for b in range(buffers)] + [at(b, 1) for b in range(buffers)]


def whole(shape):
    return pl.BlockSpec(shape, lambda i, index: (0,) * len(shape))


def moving(width):
    return pl.BlockSpec((width, STEP), lambda i, index: (0, i))


def estimate(rows, width, columns):
    return pl.CostEstimate(
        flops=2 * 4 * rows * width * columns,
        transcendentals=rows * columns,
        bytes_accessed=4 * (rows + width) * columns,
    )


def image_part(start, slabs, index, half, counts, row_log, col):
    buffers, rows, width = len(slabs), counts.shape[0], start.shape[0]
    columns = slabs[0].shape[1]
    blocks, per_block = columns // half, half // STEP
    return pl.pallas_call(
        functools.partial(image_kernel, buffers),
        out_shape=jax.ShapeDtypeStruct(start.shape, jnp.float32),
        grid_spec=pltpu.PrefetchScalarGridSpec(
            num_scalar_prefetch=1,
            grid=(columns // STEP,),
            in_specs=[whole(row_log.shape), whole(start.shape)]
            + counts_specs(buffers, blocks, per_block, rows)
            + [moving(width)] * buffers,
            out_specs=whole(start.shape),
            scratch_shapes=[pltpu.VMEM((2 * width, 2 * rows), jnp.float32)],
        ),
        cost_estimate=estimate(rows, width, columns * buffers),
        name="image_part",
    )(index, row_log, start, *[counts] * buffers, *[col] * buffers, *slabs)


def columns_part(image, index, buffers, half, counts, row_log, col, addends=()):
    rows, width = counts.shape[0], image.shape[0]
    blocks, per_block = index.shape[0] // buffers, half // STEP
    columns = blocks * half
    return pl.pallas_call(
        functools.partial(columns_kernel, buffers, len(addends) > 0),
        out_shape=[jax.ShapeDtypeStruct((width, columns), jnp.float32)] * buffers,
        grid_spec=pltpu.PrefetchScalarGridSpec(
            num_scalar_prefetch=1,
            grid=(columns // STEP,),
            in_specs=[whole(row_log.shape), whole(image.shape)]
            + counts_specs(buffers, blocks, per_block, rows)
            + [moving(width)] * len(addends),
            out_specs=[moving(width)] * buffers,
        ),
        cost_estimate=estimate(rows, width, columns * buffers),
        name="columns_part",
    )(index, row_log, image, *[counts] * buffers, *[col] * buffers, *addends)


def per_device(counts, row_total, col_total, grand_total, sketch):
    row_log = (jnp.log(grand_total[0]) - jnp.log(row_total))[:, None]
    col = col_total[None, :]
    rows, width = counts.shape[0], sketch.shape[1]
    slab = sketch.T
    half = slab.shape[1] // 2
    z, y = lax.axis_index(Z), lax.axis_index(Y)
    size = lax.axis_size(Y)

    def block(part, dz, dy):
        return (((z + dz) % size) * size + (y + dy) % size) * 2 + part

    def blocks_a(pairs):
        return [block(0, along, across) for along, across in pairs]

    def blocks_b(pairs):
        return [block(1, across, along) for along, across in pairs]

    def indices(*lists):
        return jnp.stack([i for one in lists for i in one]).astype(jnp.int32)

    args = (half, counts, row_log, col)

    a, b = slab[:, :half], slab[:, half:]
    a_m, a_p = shift(a, Z, 1), shift(a, Z, -1)
    b_m, b_p = shift(b, Y, 1), shift(b, Y, -1)
    a_2, b_2 = shift(a, Z, 2), shift(b, Y, 2)
    a0, b0 = jnp.concatenate([a, a_m], axis=1), jnp.concatenate([b, b_m], axis=1)
    a0_m, a0_p = shift(a0, Y, 1), shift(a0, Y, -1)
    b0_m, b0_p = shift(b0, Z, 1), shift(b0, Z, -1)
    a1, b1 = jnp.concatenate([a_p, a_2], axis=1), jnp.concatenate([b_p, b_2], axis=1)
    a1_p, a1_m = shift(a1, Y, -1), shift(a1, Y, 1)
    b1_p, b1_m = shift(b1, Z, -1), shift(b1, Z, 1)
    a0_2, b0_2 = shift(a0_m, Y, 1), shift(b0_m, Z, 1)
    a1_2, b1_2 = shift(a1_p, Y, -1), shift(b1_p, Z, -1)

    def first(across):
        return [(0, across), (-1, across)]

    def second(across):
        return [(1, across), (2, across)]

    image = jnp.zeros((width, rows), jnp.float32)
    image = image_part(
        image, [a0, b0, a1, b1],
        indices(blocks_a(first(0)), blocks_b(first(0)), blocks_a(second(0)), blocks_b(second(0))), *args,
    )
    image = image_part(
        image, [a0_m, b0_m, a0_p, b0_p],
        indices(blocks_a(first(-1)), blocks_b(first(-1)), blocks_a(first(1)), blocks_b(first(1))), *args,
    )
    image = image_part(
        image, [a1_p, b1_p, a1_m, b1_m],
        indices(blocks_a(second(1)), blocks_b(second(1)), blocks_a(second(-1)), blocks_b(second(-1))), *args,
    )
    image = image_part(
        image, [a0_2, b0_2, a1_2, b1_2],
        indices(blocks_a(first(2)), blocks_b(first(2)), blocks_a(second(2)), blocks_b(second(2))), *args,
    )
    for bit in (1, 2, 4):
        image = add_partner(image, "col", bit)

    def near(across):
        return [(0, across), (1, across)]

    def far(across):
        return [(-1, across), (2, across)]

    far_index = indices(blocks_a(near(2)), blocks_b(near(2)), blocks_a(far(2)), blocks_b(far(2)))
    a0_f, b0_f, a1_f, b1_f = columns_part(image, far_index, 4, *args)
    image, a0_f, b0_f, a1_f, b1_f = lax.optimization_barrier((image, a0_f, b0_f, a1_f, b1_f))
    a0_in, b0_in = shift(a0_f, Y, 1), shift(b0_f, Z, 1)
    a1_in, b1_in = shift(a1_f, Y, -1), shift(b1_f, Z, -1)

    direct_index = indices(blocks_a(far(1)), blocks_b(far(1)), blocks_a(near(-1)), blocks_b(near(-1)))
    a1_d, b1_d, a0_d, b0_d = columns_part(image, direct_index, 4, *args)
    image, a1_d, b1_d, a0_d, b0_d = lax.optimization_barrier((image, a1_d, b1_d, a0_d, b0_d))
    a1_c, b1_c = shift(a1_d, Y, 1), shift(b1_d, Z, 1)
    a0_c, b0_c = shift(a0_d, Y, -1), shift(b0_d, Z, -1)

    passed_index = indices(blocks_a(near(1)), blocks_b(near(1)), blocks_a(far(-1)), blocks_b(far(-1)))
    a0_s, b0_s, a1_s, b1_s = columns_part(image, passed_index, 4, *args, addends=(a0_in, b0_in, a1_in, b1_in))
    a0_e, b0_e = shift(a0_s, Y, 1), shift(b0_s, Z, 1)
    a1_e, b1_e = shift(a1_s, Y, -1), shift(b1_s, Z, -1)

    own_index = indices(blocks_a(near(0)), blocks_b(near(0)), blocks_a(far(0)), blocks_b(far(0)))
    a0_o, b0_o, a1_o, b1_o = columns_part(image, own_index, 4, *args)

    gram = jnp.dot(image, image.T, precision=lax.Precision.HIGHEST, preferred_element_type=jnp.float32)
    for axis in (Y, Z):
        for bit in (1, 2):
            gram = add_partner(gram, axis, bit)
    factor = jnp.linalg.cholesky(gram)
    inverse = jax.scipy.linalg.solve_triangular(factor, jnp.eye(width, dtype=jnp.float32), lower=True)

    def halves(*arrays):
        return [sum(x[:, at] for x in arrays) for at in (slice(0, half), slice(half, None))]

    a_own, a_up = halves(a0_o, a0_c, a0_e)
    a_down, a_far = halves(a1_o, a1_c, a1_e)
    b_own, b_up = halves(b0_o, b0_c, b0_e)
    b_down, b_far = halves(b1_o, b1_c, b1_e)
    a_sum = a_own + shift(a_far, Z, 2) + shift(a_up, Z, 1) + shift(a_down, Z, -1)
    b_sum = b_own + shift(b_far, Y, 2) + shift(b_up, Y, 1) + shift(b_down, Y, -1)
    summed = jnp.concatenate([a_sum, b_sum], axis=1)
    factors = jnp.dot(inverse, summed, precision=lax.Precision.HIGHEST, preferred_element_type=jnp.float32)
    return factors.T, factor


def solution(mesh):
    finer = Mesh(mesh.devices.reshape(4, 4, mesh.shape["col"]), ("row_0", "row_1", "col"))
    placed = (P(ROW, "col"), P(ROW), P("col"), P(), P(COL_ROW, None))
    return jax.shard_map(
        per_device, mesh=finer, in_specs=placed, out_specs=(P(COL_ROW, None), P()), check_vma=False
    )
```

```python
import functools

import jax
import jax.numpy as jnp
from jax import lax
from jax.experimental import pallas as pl
from jax.experimental.pallas import tpu as pltpu
from jax.sharding import Mesh
from jax.sharding import PartitionSpec as P


ROW = ("row_0", "row_1")
COL_ROW = ("col", "row_0", "row_1")
Z, Y = ROW
MIB = 1024 * 1024
TILE = 16
EARLY = 8


def shift(array, axis, by):
    size, cols = lax.axis_size(axis), lax.axis_size("col")

    def target(z, y, c):
        step = -by if c % 2 else by
        z, y = ((z + step) % size, y) if axis == Z else (z, (y + step) % size)
        return (z * size + y) * cols + c

    places = [(z, y, c) for z in range(size) for y in range(size) for c in range(cols)]
    return lax.ppermute(array, (Z, Y, "col"), [(at, target(*place)) for at, place in enumerate(places)])


def partner(array, axis, bit):
    size = lax.axis_size(axis)
    return lax.ppermute(array, axis, [(i, i ^ bit) for i in range(size)])


def over_col(array):
    array = array + partner(array, "col", 1)
    near, far, both = [partner(array, "col", bit) for bit in (2, 4, 6)]
    return (array + near) + (far + both)


def from_row(array, bit):
    cols = lax.axis_size("col")
    rows = lax.axis_size(Z) * lax.axis_size(Y)
    pairs = [(r * cols + c, (r ^ (2 * c + bit)) * cols + c) for r in range(rows) for c in range(cols)]
    return lax.ppermute(array, (Z, Y, "col"), pairs)


def two_parts(x):
    high = x.astype(jnp.bfloat16)
    low = (x - high.astype(jnp.float32)).astype(jnp.bfloat16)
    return high, low


def ppmi_kernel(first, tile, row_ref, col_ref, counts_ref, *refs):
    out_ref, counts, ppmi, sems = refs[-4:]
    blocks, rows, half = counts.shape

    def in_copy(at):
        columns = pl.ds(pl.multiple_of((first + at) * half, half), half)
        return pltpu.make_async_copy(counts_ref.at[:, columns], counts.at[at], sems.at[0, at])

    def out_copy(at):
        return pltpu.make_async_copy(ppmi.at[at], out_ref.at[first + at], sems.at[1, at])

    for at in range(blocks):
        in_copy(at).start()

    @pl.loop(0, blocks)
    def _(at):
        col_log = jnp.log(col_ref[:, pl.ds(pl.multiple_of((first + at) * half, half), half)])
        in_copy(at).wait()
        for row in range(0, rows, tile):
            logs = jnp.log(counts[at, row : row + tile, :].astype(jnp.float32))
            high, low = two_parts(jnp.maximum(logs + (row_ref[row : row + tile, :] - col_log), 0.0))
            ppmi[at, row : row + tile, :] = high
            ppmi[at, rows + row : rows + row + tile, :] = low
        out_copy(at).start()

    @pl.loop(0, blocks)
    def _(at):
        out_copy(at).wait()


def ppmi_blocks(counts, row_log, col, half, first, blocks, earlier=()):
    rows, columns = counts.shape
    return pl.pallas_call(
        functools.partial(ppmi_kernel, first, TILE),
        out_shape=jax.ShapeDtypeStruct((columns // half, 2 * rows, half), jnp.bfloat16),
        in_specs=[pl.BlockSpec(memory_space=pltpu.VMEM)] * 2 + any_space(1 + len(earlier)),
        out_specs=pl.BlockSpec(memory_space=pl.ANY),
        scratch_shapes=[
            pltpu.VMEM((blocks, rows, half), jnp.int32),
            pltpu.VMEM((blocks, 2 * rows, half), jnp.bfloat16),
            pltpu.SemaphoreType.DMA((2, blocks)),
        ],
        input_output_aliases={3: 0} if earlier else {},
        cost_estimate=pl.CostEstimate(
            flops=8 * rows * half * blocks,
            transcendentals=rows * half * blocks,
            bytes_accessed=8 * rows * half * blocks,
        ),
        compiler_params=pltpu.CompilerParams(vmem_limit_bytes=48 * MIB),
        name="ppmi_blocks",
    )(row_log, col, counts, *earlier)


def block_of(place_ref, part, dz, dy, size):
    z = lax.rem(place_ref[0] + dz * place_ref[2] + size, size)
    y = lax.rem(place_ref[1] + dy * place_ref[2] + size, size)
    return (z * size + y) * 2 + part


def image_kernel(blocks, size, place_ref, ppmi_ref, start_ref, *refs):
    slabs, (out_ref, ppmi, slab, total, sems) = refs[:-5], refs[-5:]
    width, half = slab.shape[1:]
    rows = start_ref.shape[1]
    parts = [(ref, part) for ref in slabs for part in range(ref.shape[1] // half)]

    def ppmi_copy(at, source):
        return pltpu.make_async_copy(ppmi_ref.at[source], ppmi.at[at], sems.at[0, at])

    def slab_copy(at, ref, part):
        return pltpu.make_async_copy(ref.at[:, pl.ds(part * half, half)], slab.at[at], sems.at[1, at])

    for at, where in enumerate(blocks):
        ppmi_copy(at, block_of(place_ref, *where, size)).start()
        slab_copy(at, *parts[at]).start()
    total[...] = jnp.zeros_like(total)

    @pl.loop(0, len(blocks))
    def _(at):
        ppmi_copy(at, 0).wait()
        slab_copy(at, slabs[0], 0).wait()
        parts = jnp.concatenate(two_parts(slab[at]), axis=0)
        total[...] += lax.dot_general(
            parts, ppmi[at], (((1,), (1,)), ((), ())), preferred_element_type=jnp.float32
        )

    cross = total[:width, rows:] + total[width:, :rows]
    out_ref[...] = start_ref[...] + (total[:width, :rows] + cross)


def parts_of(refs, half):
    return [ref.at[:, pl.ds(part * half, half)] for ref in refs for part in range(ref.shape[1] // half)]


def columns_kernel(blocks, size, buffers, place_ref, ppmi_ref, image_ref, *refs):
    ppmi, held, ready, left, sems = refs[-5:]
    width, half = ready.shape[1:]
    count = len(blocks)
    addends = parts_of(refs[: len(refs) - 5 - buffers], half)
    outs = parts_of(refs[len(refs) - 5 - buffers : -5], half)

    def ppmi_copy(at, source):
        return pltpu.make_async_copy(ppmi_ref.at[source], ppmi.at[at], sems.at[at])

    def held_copy(at):
        return pltpu.make_async_copy(addends[at], held.at[at], sems.at[2 * count + at])

    def out_copy(at):
        return pltpu.make_async_copy(ready.at[at], outs[at], sems.at[count + at])

    for at, where in enumerate(blocks):
        ppmi_copy(at, block_of(place_ref, *where, size)).start()
        for held_at in range(at, len(addends), count):
            held_copy(held_at).start()
    high, low = two_parts(image_ref[...])
    rows = high.shape[1]
    left[:width, :rows] = high
    left[:width, rows:] = high
    left[width:, :rows] = low
    left[width:, rows:] = jnp.zeros_like(low)
    for at in range(count):
        ppmi_copy(at, 0).wait()
        product = jnp.dot(left[...], ppmi[at], preferred_element_type=jnp.float32)
        value = product[:width] + product[width:]
        for held_at in range(at, len(addends), count):
            held_copy(held_at).wait()
            value = value + held[held_at]
        ready[at] = value
        out_copy(at).start()
    for at in range(count):
        out_copy(at).wait()


def factors_kernel(inverse_ref, *refs):
    out_ref, held, ready, sems = refs[-4:]
    half = held.shape[2]
    parts = [ref.at[:, pl.ds(0, half)] for ref in refs[:-4]]
    outs = parts_of([out_ref], half)
    each = len(parts) // len(outs)

    def held_copy(at):
        return pltpu.make_async_copy(parts[at], held.at[at], sems.at[at])

    def out_copy(at):
        return pltpu.make_async_copy(ready.at[at], outs[at], sems.at[len(parts) + at])

    for at in range(len(parts)):
        held_copy(at).start()
    for at in range(len(outs)):
        mine = range(at * each, (at + 1) * each)
        for held_at in mine:
            held_copy(held_at).wait()
        summed = sum(held[held_at] for held_at in mine)
        ready[at] = jnp.dot(
            inverse_ref[...], summed, precision=lax.Precision.HIGHEST, preferred_element_type=jnp.float32
        )
        out_copy(at).start()
    for at in range(len(outs)):
        out_copy(at).wait()


def solved(inverse, parts, outs, half):
    width = inverse.shape[0]
    return pl.pallas_call(
        factors_kernel,
        out_shape=jax.ShapeDtypeStruct((width, outs * half), jnp.float32),
        in_specs=[pl.BlockSpec(memory_space=pltpu.VMEM)] + any_space(len(parts)),
        out_specs=pl.BlockSpec(memory_space=pl.ANY),
        scratch_shapes=[
            pltpu.VMEM((len(parts), width, half), jnp.float32),
            pltpu.VMEM((outs, width, half), jnp.float32),
            pltpu.SemaphoreType.DMA((len(parts) + outs,)),
        ],
        cost_estimate=estimate(outs, width, width, half),
        compiler_params=pltpu.CompilerParams(vmem_limit_bytes=63 * MIB),
        name="solved",
    )(inverse, *parts)


def estimate(blocks, rows, width, half):
    columns = blocks * half
    return pl.CostEstimate(
        flops=2 * 4 * rows * width * columns, transcendentals=0, bytes_accessed=4 * (rows + width) * columns
    )


def any_space(count):
    return [pl.BlockSpec(memory_space=pl.ANY)] * count


def image_part(start, slabs, blocks, place, ppmi, size):
    width, rows = start.shape
    half = ppmi.shape[2]
    return pl.pallas_call(
        functools.partial(image_kernel, blocks, size),
        out_shape=jax.ShapeDtypeStruct(start.shape, jnp.float32),
        in_specs=[pl.BlockSpec(memory_space=pltpu.SMEM)] + any_space(1)
        + [pl.BlockSpec(memory_space=pltpu.VMEM)] + any_space(len(slabs)),
        out_specs=pl.BlockSpec(memory_space=pltpu.VMEM),
        scratch_shapes=[
            pltpu.VMEM((len(blocks), 2 * rows, half), jnp.bfloat16),
            pltpu.VMEM((len(blocks), width, half), jnp.float32),
            pltpu.VMEM((2 * width, 2 * rows), jnp.float32),
            pltpu.SemaphoreType.DMA((2, len(blocks))),
        ],
        cost_estimate=estimate(len(blocks), rows, width, half),
        compiler_params=pltpu.CompilerParams(vmem_limit_bytes=48 * MIB),
        name="image_part",
    )(place, ppmi, start, *slabs)


def columns_part(image, blocks, buffers, place, ppmi, size, addends=()):
    width, rows = image.shape
    half = ppmi.shape[2]
    count = len(blocks)
    groups = sum(x.shape[1] for x in addends) // (count * half)
    return pl.pallas_call(
        functools.partial(columns_kernel, blocks, size, buffers),
        out_shape=[jax.ShapeDtypeStruct((width, count // buffers * half), jnp.float32)] * buffers,
        in_specs=[pl.BlockSpec(memory_space=pltpu.SMEM)] + any_space(1)
        + [pl.BlockSpec(memory_space=pltpu.VMEM)] + any_space(len(addends)),
        out_specs=[pl.BlockSpec(memory_space=pltpu.HBM)] * buffers,
        scratch_shapes=[
            pltpu.VMEM((count, 2 * rows, half), jnp.bfloat16),
            pltpu.VMEM((max(1, count * groups), width, half), jnp.float32),
            pltpu.VMEM((count, width, half), jnp.float32),
            pltpu.VMEM((2 * width, 2 * rows), jnp.bfloat16),
            pltpu.SemaphoreType.DMA((count * (2 + groups),)),
        ],
        cost_estimate=estimate(count, rows, width, half),
        compiler_params=pltpu.CompilerParams(vmem_limit_bytes=63 * MIB),
        name="columns_part",
    )(place, ppmi, image, *addends)


def per_device(counts, row_total, col_total, grand_total, sketch):
    row_log = (jnp.log(grand_total[0]) - jnp.log(row_total))[:, None]
    col = col_total[None, :]
    rows, width = counts.shape[0], sketch.shape[1]
    slab = sketch.T
    half = slab.shape[1] // 2
    z, y = lax.axis_index(Z), lax.axis_index(Y)
    size = lax.axis_size(Y)

    def blocks_a(pairs):
        return [(0, along, across) for along, across in pairs]

    def blocks_b(pairs):
        return [(1, across, along) for along, across in pairs]

    place = jnp.stack([z, y, 1 - 2 * (lax.axis_index("col") % 2)]).astype(jnp.int32)
    ppmi = ppmi_blocks(counts, row_log, col, half, 0, EARLY)
    ppmi = ppmi_blocks(counts, row_log, col, half, EARLY, counts.shape[1] // half - EARLY, (ppmi,))
    args = (place, ppmi, size)

    a, b = slab[:, :half], slab[:, half:]
    a_m, a_p = shift(a, Z, 1), shift(a, Z, -1)
    b_m, b_p = shift(b, Y, 1), shift(b, Y, -1)
    a_2, b_2 = shift(a_m, Z, 1), shift(b_p, Y, -1)
    a0, b0 = jnp.concatenate([a, a_m], axis=1), jnp.concatenate([b, b_m], axis=1)
    a0_m, a0_p = shift(a0, Y, 1), shift(a0, Y, -1)
    b0_m, b0_p = shift(b0, Z, 1), shift(b0, Z, -1)
    a1, b1 = jnp.concatenate([a_p, a_2], axis=1), jnp.concatenate([b_p, b_2], axis=1)
    a1_p, a1_m = shift(a1, Y, -1), shift(a1, Y, 1)
    b1_p, b1_m = shift(b1, Z, -1), shift(b1, Z, 1)
    a0_2, b0_2 = shift(a0_m, Y, 1), shift(b0_m, Z, 1)
    a1_2, b1_2 = shift(a1_p, Y, -1), shift(b1_p, Z, -1)

    def first(across):
        return [(0, across), (-1, across)]

    def second(across):
        return [(1, across), (2, across)]

    image = jnp.zeros((width, rows), jnp.float32)
    where = blocks_a(first(0)) + blocks_b(first(0)) + blocks_a(second(0)) + blocks_b(second(0))
    image = image_part(image, [a0, b0, a1, b1], where, *args)
    where = blocks_a(first(-1)) + blocks_b(first(-1)) + blocks_a(first(1)) + blocks_b(first(1))
    image = image_part(image, [a0_m, b0_m, a0_p, b0_p], where, *args)
    where = blocks_a(second(1)) + blocks_b(second(1)) + blocks_a(second(-1)) + blocks_b(second(-1))
    image = image_part(image, [a1_p, b1_p, a1_m, b1_m], where, *args)
    where = blocks_a(first(2)) + blocks_b(first(2)) + blocks_a(second(2)) + blocks_b(second(2))
    image = image_part(image, [a0_2, b0_2, a1_2, b1_2], where, *args)
    image = over_col(image)

    gram = jnp.dot(image, image.T, precision=lax.Precision.HIGHEST, preferred_element_type=jnp.float32)
    gram = from_row(gram, 0) + from_row(gram, 1)
    gram = over_col(gram)
    factor = jnp.linalg.cholesky(gram)
    inverse = jax.scipy.linalg.solve_triangular(factor, jnp.eye(width, dtype=jnp.float32), lower=True)

    def near(across):
        return [(0, across), (1, across)]

    def far(across):
        return [(-1, across), (2, across)]

    where = blocks_a(near(2)) + blocks_b(near(2)) + blocks_a(far(2)) + blocks_b(far(2))
    a0_f, b0_f, a1_f, b1_f = columns_part(image, where, 4, *args)
    a0_in, b0_in = shift(a0_f, Y, 1), shift(b0_f, Z, 1)
    a1_in, b1_in = shift(a1_f, Y, -1), shift(b1_f, Z, -1)
    where = blocks_a(far(1)) + blocks_b(far(1)) + blocks_a(near(-1)) + blocks_b(near(-1))
    a1_d, b1_d, a0_d, b0_d = columns_part(image, where, 4, *args)
    a1_c, b1_c = shift(a1_d, Y, 1), shift(b1_d, Z, 1)
    a0_c, b0_c = shift(a0_d, Y, -1), shift(b0_d, Z, -1)
    where = blocks_a(near(1)) + blocks_b(near(1)) + blocks_a(far(-1)) + blocks_b(far(-1))
    a0_s, b0_s, a1_s, b1_s = columns_part(image, where, 4, *args, addends=(a0_in, b0_in, a1_in, b1_in))
    a0_e, b0_e = shift(a0_s, Y, 1), shift(b0_s, Z, 1)
    a1_e, b1_e = shift(a1_s, Y, -1), shift(b1_s, Z, -1)

    where = blocks_a(near(0)) + blocks_b(near(0)) + blocks_a(far(0)) + blocks_b(far(0))
    a0_o, b0_o, a1_o, b1_o = columns_part(image, where, 4, *args, addends=(a0_c, b0_c, a1_c, b1_c))

    def halves(x, y):
        return [x[:, at] + y[:, at] for at in (slice(0, half), slice(half, None))]

    a_down, a_far = halves(a1_o, a1_e)
    b_down, b_far = halves(b1_o, b1_e)
    a_up, b_up = halves(a0_o, a0_e)[1], halves(b0_o, b0_e)[1]
    a_parts = [a0_o, a0_e, shift(a_far, Z, 2), shift(a_down, Z, -1), shift(a_up, Z, 1)]
    b_parts = [b0_o, b0_e, shift(b_far, Y, 2), shift(b_down, Y, -1), shift(b_up, Y, 1)]
    factors = solved(inverse, a_parts + b_parts, 2, half)
    return factors.T, factor


def solution(mesh):
    finer = Mesh(mesh.devices.reshape(4, 4, mesh.shape["col"]), ("row_0", "row_1", "col"))
    placed = (P(ROW, "col"), P(ROW), P("col"), P(), P(COL_ROW, None))

    return jax.shard_map(per_device, mesh=finer, in_specs=placed, out_specs=(P(COL_ROW, None), P()), check_vma=False)
```

```python
import functools

import jax
import jax.numpy as jnp
from jax import lax
from jax.experimental import pallas as pl
from jax.experimental.pallas import tpu as pltpu
from jax.sharding import Mesh
from jax.sharding import PartitionSpec as P


ROW = ("row_0", "row_1")
COL_ROW = ("col", "row_0", "row_1")
Z, Y = ROW
MIB = 1024 * 1024
TILE = 16
EARLY = 8


def shift(array, axis, by):
    size, cols = lax.axis_size(axis), lax.axis_size("col")

    def target(z, y, c):
        step = -by if c % 2 else by
        z, y = ((z + step) % size, y) if axis == Z else (z, (y + step) % size)
        return (z * size + y) * cols + c

    places = [(z, y, c) for z in range(size) for y in range(size) for c in range(cols)]
    return lax.ppermute(array, (Z, Y, "col"), [(at, target(*place)) for at, place in enumerate(places)])


def partner(array, axis, bit):
    size = lax.axis_size(axis)
    return lax.ppermute(array, axis, [(i, i ^ bit) for i in range(size)])


def over_col(array):
    array = array + partner(array, "col", 1)
    near, far, both = [partner(array, "col", bit) for bit in (2, 4, 6)]
    return (array + near) + (far + both)


def from_row(array, bit):
    cols = lax.axis_size("col")
    rows = lax.axis_size(Z) * lax.axis_size(Y)
    pairs = [(r * cols + c, (r ^ (2 * c + bit)) * cols + c) for r in range(rows) for c in range(cols)]
    return lax.ppermute(array, (Z, Y, "col"), pairs)


def two_parts(x):
    high = x.astype(jnp.bfloat16)
    low = (x - high.astype(jnp.float32)).astype(jnp.bfloat16)
    return high, low


def ppmi_kernel(first, tile, row_ref, col_ref, counts_ref, *refs):
    out_ref, counts, ppmi, sems = refs[-4:]
    blocks, rows, half = counts.shape

    def in_copy(at):
        columns = pl.ds(pl.multiple_of((first + at) * half, half), half)
        return pltpu.make_async_copy(counts_ref.at[:, columns], counts.at[at], sems.at[0, at])

    def out_copy(at):
        return pltpu.make_async_copy(ppmi.at[at], out_ref.at[first + at], sems.at[1, at])

    for at in range(blocks):
        in_copy(at).start()

    @pl.loop(0, blocks)
    def _(at):
        col_log = jnp.log(col_ref[:, pl.ds(pl.multiple_of((first + at) * half, half), half)])
        in_copy(at).wait()
        for row in range(0, rows, tile):
            logs = jnp.log(counts[at, row : row + tile, :].astype(jnp.float32))
            high, low = two_parts(jnp.maximum(logs + (row_ref[row : row + tile, :] - col_log), 0.0))
            ppmi[at, row : row + tile, :] = high
            ppmi[at, rows + row : rows + row + tile, :] = low
        out_copy(at).start()

    @pl.loop(0, blocks)
    def _(at):
        out_copy(at).wait()


def ppmi_blocks(counts, row_log, col, half, first, blocks, earlier=()):
    rows, columns = counts.shape
    return pl.pallas_call(
        functools.partial(ppmi_kernel, first, TILE),
        out_shape=jax.ShapeDtypeStruct((columns // half, 2 * rows, half), jnp.bfloat16),
        in_specs=[pl.BlockSpec(memory_space=pltpu.VMEM)] * 2 + any_space(1 + len(earlier)),
        out_specs=pl.BlockSpec(memory_space=pl.ANY),
        scratch_shapes=[
            pltpu.VMEM((blocks, rows, half), jnp.int32),
            pltpu.VMEM((blocks, 2 * rows, half), jnp.bfloat16),
            pltpu.SemaphoreType.DMA((2, blocks)),
        ],
        input_output_aliases={3: 0} if earlier else {},
        cost_estimate=pl.CostEstimate(
            flops=8 * rows * half * blocks,
            transcendentals=rows * half * blocks,
            bytes_accessed=8 * rows * half * blocks,
        ),
        compiler_params=pltpu.CompilerParams(vmem_limit_bytes=48 * MIB),
        name="ppmi_blocks",
    )(row_log, col, counts, *earlier)


def block_of(place_ref, part, dz, dy, size):
    z = lax.rem(place_ref[0] + dz * place_ref[2] + size, size)
    y = lax.rem(place_ref[1] + dy * place_ref[2] + size, size)
    return (z * size + y) * 2 + part


def image_kernel(blocks, size, place_ref, ppmi_ref, start_ref, *refs):
    slabs, (out_ref, ppmi, slab, total, sems) = refs[:-5], refs[-5:]
    width, half = slab.shape[1:]
    rows = start_ref.shape[1]
    parts = [(ref, part) for ref in slabs for part in range(ref.shape[1] // half)]

    def ppmi_copy(at, source):
        return pltpu.make_async_copy(ppmi_ref.at[source], ppmi.at[at], sems.at[0, at])

    def slab_copy(at, ref, part):
        return pltpu.make_async_copy(ref.at[:, pl.ds(part * half, half)], slab.at[at], sems.at[1, at])

    for at, where in enumerate(blocks):
        ppmi_copy(at, block_of(place_ref, *where, size)).start()
        slab_copy(at, *parts[at]).start()
    total[...] = jnp.zeros_like(total)

    @pl.loop(0, len(blocks))
    def _(at):
        ppmi_copy(at, 0).wait()
        slab_copy(at, slabs[0], 0).wait()
        parts = jnp.concatenate(two_parts(slab[at]), axis=0)
        total[...] += lax.dot_general(
            parts, ppmi[at], (((1,), (1,)), ((), ())), preferred_element_type=jnp.float32
        )

    cross = total[:width, rows:] + total[width:, :rows]
    out_ref[...] = start_ref[...] + (total[:width, :rows] + cross)


def parts_of(refs, half):
    return [ref.at[:, pl.ds(part * half, half)] for ref in refs for part in range(ref.shape[1] // half)]


def columns_kernel(blocks, size, buffers, place_ref, ppmi_ref, image_ref, *refs):
    ppmi, held, ready, left, sems = refs[-5:]
    width, half = ready.shape[1:]
    count = len(blocks)
    addends = parts_of(refs[: len(refs) - 5 - buffers], half)
    outs = parts_of(refs[len(refs) - 5 - buffers : -5], half)

    def ppmi_copy(at, source):
        return pltpu.make_async_copy(ppmi_ref.at[source], ppmi.at[at], sems.at[at])

    def held_copy(at):
        return pltpu.make_async_copy(addends[at], held.at[at], sems.at[2 * count + at])

    def out_copy(at):
        return pltpu.make_async_copy(ready.at[at], outs[at], sems.at[count + at])

    for at, where in enumerate(blocks):
        ppmi_copy(at, block_of(place_ref, *where, size)).start()
        for held_at in range(at, len(addends), count):
            held_copy(held_at).start()
    high, low = two_parts(image_ref[...])
    rows = high.shape[1]
    left[:width, :rows] = high
    left[:width, rows:] = high
    left[width:, :rows] = low
    left[width:, rows:] = jnp.zeros_like(low)
    for at in range(count):
        ppmi_copy(at, 0).wait()
        product = jnp.dot(left[...], ppmi[at], preferred_element_type=jnp.float32)
        value = product[:width] + product[width:]
        for held_at in range(at, len(addends), count):
            held_copy(held_at).wait()
            value = value + held[held_at]
        ready[at] = value
        out_copy(at).start()
    for at in range(count):
        out_copy(at).wait()


def factors_kernel(inverse_ref, *refs):
    out_ref, held, ready, sems = refs[-4:]
    half = held.shape[2]
    parts = [ref.at[:, pl.ds(0, half)] for ref in refs[:-4]]
    outs = parts_of([out_ref], half)
    each = len(parts) // len(outs)

    def held_copy(at):
        return pltpu.make_async_copy(parts[at], held.at[at], sems.at[at])

    def out_copy(at):
        return pltpu.make_async_copy(ready.at[at], outs[at], sems.at[len(parts) + at])

    for at in range(len(parts)):
        held_copy(at).start()
    for at in range(len(outs)):
        mine = range(at * each, (at + 1) * each)
        for held_at in mine:
            held_copy(held_at).wait()
        summed = sum(held[held_at] for held_at in mine)
        ready[at] = jnp.dot(
            inverse_ref[...], summed, precision=lax.Precision.HIGHEST, preferred_element_type=jnp.float32
        )
        out_copy(at).start()
    for at in range(len(outs)):
        out_copy(at).wait()


def solved(inverse, parts, outs, half):
    width = inverse.shape[0]
    return pl.pallas_call(
        factors_kernel,
        out_shape=jax.ShapeDtypeStruct((width, outs * half), jnp.float32),
        in_specs=[pl.BlockSpec(memory_space=pltpu.VMEM)] + any_space(len(parts)),
        out_specs=pl.BlockSpec(memory_space=pl.ANY),
        scratch_shapes=[
            pltpu.VMEM((len(parts), width, half), jnp.float32),
            pltpu.VMEM((outs, width, half), jnp.float32),
            pltpu.SemaphoreType.DMA((len(parts) + outs,)),
        ],
        cost_estimate=estimate(outs, width, width, half),
        compiler_params=pltpu.CompilerParams(vmem_limit_bytes=63 * MIB),
        name="solved",
    )(inverse, *parts)


def estimate(blocks, rows, width, half):
    columns = blocks * half
    return pl.CostEstimate(
        flops=2 * 4 * rows * width * columns, transcendentals=0, bytes_accessed=4 * (rows + width) * columns
    )


def any_space(count):
    return [pl.BlockSpec(memory_space=pl.ANY)] * count


def image_part(start, slabs, blocks, place, ppmi, size):
    width, rows = start.shape
    half = ppmi.shape[2]
    return pl.pallas_call(
        functools.partial(image_kernel, blocks, size),
        out_shape=jax.ShapeDtypeStruct(start.shape, jnp.float32),
        in_specs=[pl.BlockSpec(memory_space=pltpu.SMEM)] + any_space(1)
        + [pl.BlockSpec(memory_space=pltpu.VMEM)] + any_space(len(slabs)),
        out_specs=pl.BlockSpec(memory_space=pltpu.VMEM),
        scratch_shapes=[
            pltpu.VMEM((len(blocks), 2 * rows, half), jnp.bfloat16),
            pltpu.VMEM((len(blocks), width, half), jnp.float32),
            pltpu.VMEM((2 * width, 2 * rows), jnp.float32),
            pltpu.SemaphoreType.DMA((2, len(blocks))),
        ],
        cost_estimate=estimate(len(blocks), rows, width, half),
        compiler_params=pltpu.CompilerParams(vmem_limit_bytes=48 * MIB),
        name="image_part",
    )(place, ppmi, start, *slabs)


def columns_part(image, blocks, buffers, place, ppmi, size, addends=(), grant=63):
    width, rows = image.shape
    half = ppmi.shape[2]
    count = len(blocks)
    groups = sum(x.shape[1] for x in addends) // (count * half)
    return pl.pallas_call(
        functools.partial(columns_kernel, blocks, size, buffers),
        out_shape=[jax.ShapeDtypeStruct((width, count // buffers * half), jnp.float32)] * buffers,
        in_specs=[pl.BlockSpec(memory_space=pltpu.SMEM)] + any_space(1)
        + [pl.BlockSpec(memory_space=pltpu.VMEM)] + any_space(len(addends)),
        out_specs=[pl.BlockSpec(memory_space=pltpu.HBM)] * buffers,
        scratch_shapes=[
            pltpu.VMEM((count, 2 * rows, half), jnp.bfloat16),
            pltpu.VMEM((max(1, count * groups), width, half), jnp.float32),
            pltpu.VMEM((count, width, half), jnp.float32),
            pltpu.VMEM((2 * width, 2 * rows), jnp.bfloat16),
            pltpu.SemaphoreType.DMA((count * (2 + groups),)),
        ],
        cost_estimate=estimate(count, rows, width, half),
        compiler_params=pltpu.CompilerParams(vmem_limit_bytes=grant * MIB),
        name="columns_part",
    )(place, ppmi, image, *addends)


def per_device(counts, row_total, col_total, grand_total, sketch):
    row_log = (jnp.log(grand_total[0]) - jnp.log(row_total))[:, None]
    col = col_total[None, :]
    rows, width = counts.shape[0], sketch.shape[1]
    slab = sketch.T
    half = slab.shape[1] // 2
    z, y = lax.axis_index(Z), lax.axis_index(Y)
    size = lax.axis_size(Y)

    def blocks_a(pairs):
        return [(0, along, across) for along, across in pairs]

    def blocks_b(pairs):
        return [(1, across, along) for along, across in pairs]

    place = jnp.stack([z, y, 1 - 2 * (lax.axis_index("col") % 2)]).astype(jnp.int32)
    ppmi = ppmi_blocks(counts, row_log, col, half, 0, EARLY)
    ppmi = ppmi_blocks(counts, row_log, col, half, EARLY, counts.shape[1] // half - EARLY, (ppmi,))
    args = (place, ppmi, size)

    a, b = slab[:, :half], slab[:, half:]
    a_m, a_p = shift(a, Z, 1), shift(a, Z, -1)
    b_m, b_p = shift(b, Y, 1), shift(b, Y, -1)
    a_2, b_2 = shift(a_m, Z, 1), shift(b_p, Y, -1)
    a0, b0 = jnp.concatenate([a, a_m], axis=1), jnp.concatenate([b, b_m], axis=1)
    a0_m, a0_p = shift(a0, Y, 1), shift(a0, Y, -1)
    b0_m, b0_p = shift(b0, Z, 1), shift(b0, Z, -1)
    a1, b1 = jnp.concatenate([a_p, a_2], axis=1), jnp.concatenate([b_p, b_2], axis=1)
    a1_p, a1_m = shift(a1, Y, -1), shift(a1, Y, 1)
    b1_p, b1_m = shift(b1, Z, -1), shift(b1, Z, 1)
    a0_2, b0_2 = shift(a0_m, Y, 1), shift(b0_m, Z, 1)
    a1_2, b1_2 = shift(a1_p, Y, -1), shift(b1_p, Z, -1)

    def first(across):
        return [(0, across), (-1, across)]

    def second(across):
        return [(1, across), (2, across)]

    image = jnp.zeros((width, rows), jnp.float32)
    where = blocks_a(first(0)) + blocks_b(first(0)) + blocks_a(second(0)) + blocks_b(second(0))
    image = image_part(image, [a0, b0, a1, b1], where, *args)
    where = blocks_a(first(-1)) + blocks_b(first(-1)) + blocks_a(first(1)) + blocks_b(first(1))
    image = image_part(image, [a0_m, b0_m, a0_p, b0_p], where, *args)
    where = blocks_a(second(1)) + blocks_b(second(1)) + blocks_a(second(-1)) + blocks_b(second(-1))
    image = image_part(image, [a1_p, b1_p, a1_m, b1_m], where, *args)
    where = blocks_a(first(2)) + blocks_b(first(2)) + blocks_a(second(2)) + blocks_b(second(2))
    image = image_part(image, [a0_2, b0_2, a1_2, b1_2], where, *args)
    image = over_col(image)

    gram = jnp.dot(image, image.T, precision=lax.Precision.HIGHEST, preferred_element_type=jnp.float32)
    gram = from_row(gram, 0) + from_row(gram, 1)
    gram = over_col(gram)
    factor = jnp.linalg.cholesky(gram)
    inverse = jax.scipy.linalg.solve_triangular(factor, jnp.eye(width, dtype=jnp.float32), lower=True)

    def near(across):
        return [(0, across), (1, across)]

    def far(across):
        return [(-1, across), (2, across)]

    a0_f, b0_f = columns_part(image, blocks_a(near(2)) + blocks_b(near(2)), 2, *args, grant=48)
    a1_f, b1_f = columns_part(image, blocks_a(far(2)) + blocks_b(far(2)), 2, *args, grant=48)
    a0_in, b0_in = shift(a0_f, Y, 1), shift(b0_f, Z, 1)
    a1_in, b1_in = shift(a1_f, Y, -1), shift(b1_f, Z, -1)
    where = blocks_a(far(1)) + blocks_b(far(1)) + blocks_a(near(-1)) + blocks_b(near(-1))
    a1_d, b1_d, a0_d, b0_d = columns_part(image, where, 4, *args, grant=48)
    a1_c, b1_c = shift(a1_d, Y, 1), shift(b1_d, Z, 1)
    a0_c, b0_c = shift(a0_d, Y, -1), shift(b0_d, Z, -1)
    where = blocks_a(near(1)) + blocks_b(near(1)) + blocks_a(far(-1)) + blocks_b(far(-1))
    a0_s, b0_s, a1_s, b1_s = columns_part(image, where, 4, *args, addends=(a0_in, b0_in, a1_in, b1_in))
    a0_e, b0_e = shift(a0_s, Y, 1), shift(b0_s, Z, 1)
    a1_e, b1_e = shift(a1_s, Y, -1), shift(b1_s, Z, -1)

    where = blocks_a(near(0)) + blocks_b(near(0)) + blocks_a(far(0)) + blocks_b(far(0))
    a0_o, b0_o, a1_o, b1_o = columns_part(image, where, 4, *args, addends=(a0_c, b0_c, a1_c, b1_c))

    def halves(x, y):
        return [x[:, at] + y[:, at] for at in (slice(0, half), slice(half, None))]

    a_down, a_far = halves(a1_o, a1_e)
    b_down, b_far = halves(b1_o, b1_e)
    a_up, b_up = halves(a0_o, a0_e)[1], halves(b0_o, b0_e)[1]
    a_parts = [a0_o, a0_e, shift(a_far, Z, 2), shift(a_down, Z, -1), shift(a_up, Z, 1)]
    b_parts = [b0_o, b0_e, shift(b_far, Y, 2), shift(b_down, Y, -1), shift(b_up, Y, 1)]
    factors = solved(inverse, a_parts + b_parts, 2, half)
    return factors.T, factor


def solution(mesh):
    finer = Mesh(mesh.devices.reshape(4, 4, mesh.shape["col"]), ("row_0", "row_1", "col"))
    placed = (P(ROW, "col"), P(ROW), P("col"), P(), P(COL_ROW, None))

    return jax.shard_map(per_device, mesh=finer, in_specs=placed, out_specs=(P(COL_ROW, None), P()), check_vma=False)
```
